256 devices in a mesh: section: 2 (over core), ctx: 32 (over z, x), mp: 4 (over y).
Axes of the slice: x: 4, y: 4, z: 8, core: 2. Of those that a mesh axis runs over, the one named last changes fastest.
Arguments:
- hidden: bfloat16 [2, 4096, 4672], P('section', 'ctx', 'mp'), may hold values from -120 to 120
- query: bfloat16 [2, 4096, 2048], P('section', 'ctx', 'mp'), may hold values from -6 to 6
- keys: bfloat16 [2, 4096, 2048], P('section', 'ctx', 'mp'), may hold values from -100 to 100
- values: bfloat16 [2, 4096, 2048], P('section', 'ctx', 'mp'), may hold values from -12 to 12
- w_out: bfloat16 [2, 4672, 2048], P('section', 'ctx', 'mp'), may hold values from -0.125 to 0.125
Outputs:
- handed: bfloat16 [2, 4096, 4672], P('section', 'ctx', 'mp')
- context: bfloat16 [2, 4096, 2048], P('section', 'ctx', 'mp')
The draws below stay inside these ranges and needn't reach their ends.
All inputs are finite; a program needn't handle non-finite values.
Results may differ from the reference program's by a relative error of at most 0.0075.
Values may be sent and summed in bfloat16 or wider, within the bound.
No kernel may reach another device: no remote copies, remote signals or barrier semaphores. Data moves between devices by JAX's collectives and lax.ppermute only.
A program may use at most 128 MiB of HBM per device.

```python
import math
import jax
import jax.numpy as jnp
from jax import lax

D = 4672
HEADS = 32
HEAD_DIM = 64
SECTIONS = 2
DEC = 4096
ENC = 4096
INNER = 2048
INNER_DEV = 512
N_MP = 4


def draw_hidden(key, part):
    key_base, key_rows = jax.random.split(jax.random.fold_in(key, 11))
    columns = jnp.exp(math.log(3.0) * jnp.arange(D, dtype=jnp.float32) / (D - 1))
    base = jnp.clip(jax.random.normal(key_base, (SECTIONS, DEC, D), jnp.float32), -4.0, 4.0)
    row_scale = jnp.exp(jax.random.uniform(key_rows, (SECTIONS, DEC, 1), jnp.float32, 0.0, math.log(10.0)))
    return (base * row_scale * columns).astype(jnp.bfloat16)


def draw_keys(key, part):
    key_base = jax.random.fold_in(jax.random.fold_in(key, 23), 0)
    base = 0.3 * jnp.clip(jax.random.normal(key_base, (SECTIONS, ENC, INNER), jnp.float32), -4.0, 4.0)
    return base.astype(jnp.bfloat16)


def steps_of(key, dims, cuts, smallest, high):
    loudness = 1.0
    for dim, shards_of in cuts:
        draws = jax.random.uniform(jax.random.fold_in(jax.random.fold_in(key, 6), dim), (shards_of,), jnp.float32, smallest / len(cuts), high / len(cuts))
        loudness = loudness * jnp.repeat(jnp.exp(draws), dims[dim] // shards_of).reshape((-1,) + (1,) * (len(dims) - 1 - dim))
    return loudness


def bell_draw(own_key, shape, deviation, most, cuts=(), held_as=jnp.bfloat16):
    values = deviation * jax.random.normal(own_key, shape, jnp.float32)
    if cuts:
        values = values * steps_of(own_key, shape, cuts, -0.22, 0.18)
    return jnp.clip(values, -most, most).astype(held_as)


def setup_inputs(seed: int = 0) -> dict:
    splits = jax.random.split(jax.random.key(seed), 6)
    return {
        "hidden": draw_hidden(jax.random.fold_in(splits[5], 71), 0),
        "query": bell_draw(splits[1], (SECTIONS, DEC, INNER), 1.0, 6.0, ((0, 2), (1, 32), (2, 4))),
        "keys": draw_keys(jax.random.fold_in(splits[5], 71), 0),
        "values": bell_draw(splits[3], (SECTIONS, ENC, INNER), 3.0, 12.0, ((0, 2), (1, 32), (2, 4))),
        "w_out": bell_draw(splits[4], (SECTIONS, D, INNER), INNER ** -0.5, 0.125, ((0, 2), (1, 32), (2, 4))),
    }


def attend_head(parts):
    query_h, keys_h, values_h = parts
    scores = jnp.dot(query_h, keys_h.T, preferred_element_type=jnp.float32)
    peak = jnp.max(scores, axis=1, keepdims=True)
    expo = jnp.exp(scores - peak)
    total = jnp.sum(expo, axis=1, keepdims=True)
    return jnp.dot(expo.astype(jnp.bfloat16), values_h, preferred_element_type=jnp.float32) / total


def split_heads(matrix):
    return jnp.transpose(matrix.reshape(matrix.shape[0], HEADS, HEAD_DIM), (1, 0, 2))


def one_layer(parts):
    hidden_l, query_l, keys_l, values_l, out_w = parts
    rows_f = hidden_l.astype(jnp.float32)
    per_head = lax.map(attend_head, (split_heads(query_l), split_heads(keys_l), split_heads(values_l)))
    context = jnp.transpose(per_head, (1, 0, 2)).reshape(query_l.shape[0], HEADS * HEAD_DIM).astype(jnp.bfloat16)
    grouped = context.reshape(context.shape[0], N_MP, INNER_DEV).astype(jnp.float32)
    out_grouped = out_w.reshape(out_w.shape[0], N_MP, INNER_DEV).astype(jnp.float32)
    partial_terms = jnp.einsum("rgw,dgw->grd", grouped, out_grouped).astype(jnp.bfloat16)
    partial_terms = lax.optimization_barrier(partial_terms)
    branch = jnp.sum(partial_terms.astype(jnp.float32), axis=0)
    result = (rows_f + branch).astype(jnp.bfloat16)
    return result, context


def reference(hidden, query, keys, values, w_out):
    outputs, context = lax.map(one_layer, (hidden, query, keys, values, w_out))
    handed = jnp.roll(outputs, 1, axis=0)
    return handed, context
```

```python
import jax
import jax.numpy as jnp
import numpy as np
from jax import lax
from jax.experimental import pallas as pl
from jax.experimental.pallas import tpu as pltpu
from jax.sharding import Mesh, PartitionSpec as P

HEAD_DIM = 64
NZ, NX, NY = 8, 4, 4
Q_TILE = 256
A_ROWS = 80


F32 = jnp.float32
BF16 = jnp.bfloat16
MIB = 1 << 20


def vmem_specs(n):
    return [pl.BlockSpec(memory_space=pltpu.VMEM) for _ in range(n)]


def shift(block, axis, n, by):
    return lax.ppermute(block, axis, [(i, (i + by) % n) for i in range(n)])


def pack_kernel(q_ref, k_ref, v_ref, o_ref):
    for i, ref in enumerate((q_ref, k_ref, v_ref)):
        t = ref[0].T
        heads = t.shape[0] // HEAD_DIM
        o_ref[:, i * HEAD_DIM:(i + 1) * HEAD_DIM, :] = t.reshape(heads, HEAD_DIM, t.shape[1])


def pack(query, keys, values):
    rows, width = query.shape[1:]
    return pl.pallas_call(
        pack_kernel,
        out_shape=jax.ShapeDtypeStruct((width // HEAD_DIM, 3 * HEAD_DIM, rows), query.dtype),
        in_specs=vmem_specs(3),
        out_specs=pl.BlockSpec(memory_space=pltpu.VMEM),
        compiler_params=pltpu.CompilerParams(vmem_limit_bytes=4 * MIB),
        name="pack",
    )(query, keys, values)


def lanes(ref, lower, upper):
    return jnp.concatenate([ref[z, lower:upper, :] for z in range(ref.shape[0])], axis=1)


def block_terms(q_t, k_t, v_t, tile, peak_old):
    keys = k_t.T
    pad = jnp.ones((16, v_t.shape[1]), v_t.dtype)
    v_aug = jnp.concatenate([v_t, pad], axis=0)
    s = jnp.dot(keys, q_t[:, tile:tile + Q_TILE], preferred_element_type=F32)
    peak = jnp.max(s, axis=0, keepdims=True)
    if peak_old is not None:
        peak = jnp.maximum(peak, peak_old)
    expo = jnp.exp(s - peak).astype(BF16)
    return peak, jnp.dot(v_aug, expo, preferred_element_type=F32)


def first_kernel(r_ref, peak_ref, acc_ref):
    q_t = lanes(r_ref, 0, HEAD_DIM)
    k_t = lanes(r_ref, HEAD_DIM, 2 * HEAD_DIM)
    v_t = lanes(r_ref, 2 * HEAD_DIM, 3 * HEAD_DIM)
    for tile in range(0, q_t.shape[1], Q_TILE):
        at = slice(tile, tile + Q_TILE)
        peak, acc = block_terms(q_t, k_t, v_t, tile, None)
        peak_ref[:, at] = peak
        acc_ref[:, at] = acc


def next_kernel(last, r_ref, kv_ref, peak_ref, acc_ref, *outs):
    q_t = lanes(r_ref, 0, HEAD_DIM)
    k_t = lanes(kv_ref, 0, HEAD_DIM)
    v_t = lanes(kv_ref, HEAD_DIM, 2 * HEAD_DIM)
    for tile in range(0, q_t.shape[1], Q_TILE):
        at = slice(tile, tile + Q_TILE)
        old = peak_ref[:, at]
        peak, acc = block_terms(q_t, k_t, v_t, tile, old)
        acc = acc + acc_ref[:, at] * jnp.exp(old - peak)
        if last:
            ctx = (acc[:HEAD_DIM] / acc[HEAD_DIM:HEAD_DIM + 1]).astype(BF16)
            rows = outs[0].shape[2]
            for j in range(Q_TILE // rows):
                outs[0][tile // rows + j] = ctx[:, j * rows:(j + 1) * rows]
        else:
            outs[0][:, at] = peak
            outs[1][:, at] = acc


def attend_first(r):
    n = r.shape[0] * r.shape[2]
    return pl.pallas_call(
        first_kernel,
        out_shape=(jax.ShapeDtypeStruct((1, n), F32), jax.ShapeDtypeStruct((HEAD_DIM + 16, n), F32)),
        in_specs=vmem_specs(1),
        out_specs=tuple(vmem_specs(2)),
        compiler_params=pltpu.CompilerParams(vmem_limit_bytes=24 * MIB),
        name="attend_first",
    )(r)


def attend_next(r, kv, peak, acc, last):
    n = r.shape[0] * r.shape[2]
    if last:
        shapes = (jax.ShapeDtypeStruct((r.shape[0], HEAD_DIM, r.shape[2]), BF16),)
    else:
        shapes = (jax.ShapeDtypeStruct((1, n), F32), jax.ShapeDtypeStruct((HEAD_DIM + 16, n), F32))
    return pl.pallas_call(
        lambda *refs: next_kernel(last, *refs),
        out_shape=shapes,
        in_specs=vmem_specs(4),
        out_specs=tuple(vmem_specs(len(shapes))),
        compiler_params=pltpu.CompilerParams(vmem_limit_bytes=24 * MIB),
        name="attend_last" if last else "attend_next",
    )(r, kv, peak, acc)


def unpack_kernel(c_ref, o_ref):
    heads, dim, rows = c_ref.shape
    o_ref[0] = c_ref[...].reshape(heads * dim, rows).T


def unpack(ctx_t):
    heads, dim, rows = ctx_t.shape
    return pl.pallas_call(
        unpack_kernel,
        out_shape=jax.ShapeDtypeStruct((1, rows, heads * dim), ctx_t.dtype),
        in_specs=vmem_specs(1),
        out_specs=pl.BlockSpec(memory_space=pltpu.VMEM),
        compiler_params=pltpu.CompilerParams(vmem_limit_bytes=4 * MIB),
        name="unpack",
    )(ctx_t)


def gather_z(block, half):
    up, down = [block], [block]
    for _ in range(3):
        up.append(shift(up[-1], "z", NZ, 1))
        down.append(shift(down[-1], "z", NZ, -1))
    far = (shift(up[3][:half], "z", NZ, 1), shift(down[3][half:], "z", NZ, -1))
    return up, down, far


def gather_x(block, half):
    up = shift(block, "x", NX, 1)
    down = shift(block, "x", NX, -1)
    far = (shift(up[:half], "x", NX, 1), shift(down[half:], "x", NX, -1))
    return up, down, far


def gather_rows(w):
    pieces = []
    a, b = w[:A_ROWS], w[A_ROWS:]
    up, down, far = gather_z(a, A_ROWS // 2)
    a_z = jnp.stack(up + [jnp.concatenate(far, axis=0)] + down[:0:-1])
    xu, xd, far = gather_x(a_z, NZ // 2)
    every = list(range(NZ))
    pieces.append((a_z, [(d, 0) for d in every], 0))
    pieces.append((xu, [(d, 1) for d in every], 0))
    pieces.append((xd, [(d, 3) for d in every], 0))
    pieces.append((far[0], [(d, 2) for d in every[:NZ // 2]], 0))
    pieces.append((far[1], [(d, 2) for d in every[NZ // 2:]], 0))
    xu, xd, far = gather_x(b, 32)
    b_x = jnp.stack([b, xu, jnp.concatenate(far, axis=0), xd])
    up, down, far = gather_z(b_x, NX // 2)
    every = list(range(NX))
    for j in range(4):
        pieces.append((up[j], [(j, d) for d in every], A_ROWS))
    for j in range(1, 4):
        pieces.append((down[j], [(NZ - j, d) for d in every], A_ROWS))
    pieces.append((far[0], [(4, d) for d in every[:NX // 2]], A_ROWS))
    pieces.append((far[1], [(4, d) for d in every[NX // 2:]], A_ROWS))
    return pieces


def project_kernel(where, strip, at_ref, hidden_ref, *refs):
    contexts, ws = refs[:NY], refs[NY:NY + len(where)]
    o_ref, ctx_ref, acc_ref, full_ref = refs[NY + len(where):]
    z, x, y = at_ref[0], at_ref[1], at_ref[2]
    for d in range(NY):
        ctx_ref[(y + NY - d) % NY] = contexts[d][...].reshape(ctx_ref.shape[1:])
    acc_ref[...] = jnp.zeros(acc_ref.shape, F32)
    for (offsets, row), w_ref in zip(where, ws):
        n = w_ref.shape[1]
        for i, (dz, dx) in enumerate(offsets):
            zs = (z + NZ - dz) % NZ
            xs = (x + NX - dx) % NX
            slot = (zs % 2) * NX + xs
            part = jnp.dot(w_ref[i], ctx_ref[zs // 2], preferred_element_type=F32)
            acc_ref[slot, row:row + n, :] += part
    for slot in range(2 * NX):
        full_ref[slot * strip:(slot + 1) * strip, :] = acc_ref[slot, :strip, :]
    width = o_ref.shape[2]
    for lower in range(0, full_ref.shape[0], 128):
        upper = min(lower + 128, width)
        branch = full_ref[lower:lower + 128, :].T[:, :upper - lower]
        o_ref[0, :, lower:upper] = (hidden_ref[0, :, lower:upper].astype(F32) + branch).astype(o_ref.dtype)


def project(at, hidden, contexts, pieces, strip):
    where = [(offsets, row) for _, offsets, row in pieces]
    rows = hidden.shape[1]
    n = len(pieces)
    return pl.pallas_call(
        lambda *refs: project_kernel(where, strip, *refs),
        out_shape=jax.ShapeDtypeStruct(hidden.shape, hidden.dtype),
        in_specs=[pl.BlockSpec(memory_space=pltpu.SMEM)] + vmem_specs(1 + NY + n),
        out_specs=pl.BlockSpec(memory_space=pltpu.VMEM),
        scratch_shapes=[
            pltpu.VMEM((NY, 8 * HEAD_DIM, rows), BF16),
            pltpu.VMEM((2 * NX, 152, rows), F32),
            pltpu.VMEM((-(-hidden.shape[2] // 128) * 128, rows), F32),
        ],
        compiler_params=pltpu.CompilerParams(vmem_limit_bytes=16 * MIB),
        name="project",
    )(at, hidden, *contexts, *[p[0] for p in pieces])


def body(hidden, query, keys, values, w_out):
    at = jnp.stack([lax.axis_index("z"), lax.axis_index("x"), lax.axis_index("mp")]).astype(jnp.int32)
    strip = w_out.shape[1]
    route = [
        ((s * NZ + z) * NY + y, ((1 - s) * NZ + 2 * y + z % 2) * NY + z // 2)
        for s in range(2) for z in range(NZ) for y in range(NY)
    ]
    w_here = lax.ppermute(w_out[0], ("section", "z", "mp"), route)
    hidden_here = lax.ppermute(hidden, "section", [(0, 1), (1, 0)])

    r = lax.all_to_all(pack(query, keys, values), "z", 0, 0, tiled=True)
    kv = r[:, HEAD_DIM:, :]
    others = [shift(kv, "x", NX, d) for d in (1, 3, 2)]
    peak, acc = attend_first(r)
    for other in others[:-1]:
        peak, acc = attend_next(r, other, peak, acc, False)
    (ctx_t,) = attend_next(r, others[-1], peak, acc, True)

    own = lax.all_to_all(ctx_t, "z", 0, 0, tiled=True)
    contexts = []
    for d in range(NY):
        turn = [(s * NY + y, (1 - s) * NY + (y + d) % NY) for s in range(2) for y in range(NY)]
        contexts.append(lax.ppermute(own, ("section", "mp"), turn))
    pieces = gather_rows(w_here)
    handed = project(at, hidden_here, contexts, pieces, strip)
    return handed, unpack(own)


def solution(mesh):
    split = Mesh(mesh.devices.reshape(2, NZ, NX, NY), ("section", "z", "x", "mp"))
    spec = P("section", ("z", "x"), "mp")
    return jax.shard_map(body, mesh=split, in_specs=(spec,) * 5, out_specs=(spec, spec), check_vma=False)
```

```python
import jax
import jax.numpy as jnp
from jax import lax
from jax.experimental import pallas as pl
from jax.experimental.pallas import tpu as pltpu
from jax.sharding import Mesh, PartitionSpec as P


HEAD_DIM = 64
NZ, NX, NY = 8, 4, 4
X = ("xh", "xl")
Q_TILE = 256
K_TILE = 256


F32 = jnp.float32
BF16 = jnp.bfloat16
MIB = 1 << 20


def vmem_specs(n):
    return [pl.BlockSpec(memory_space=pltpu.VMEM) for _ in range(n)]


def shift(block, axis, n, by):
    return lax.ppermute(block, axis, [(i, (i + by) % n) for i in range(n)])


def pack_kernel(in_ref, o_ref):
    for i in range(3):
        t = in_ref[i].T
        heads = t.shape[0] // HEAD_DIM
        o_ref[:, i * HEAD_DIM:(i + 1) * HEAD_DIM, :] = t.reshape(heads, HEAD_DIM, t.shape[1])


def pack(query, keys, values):
    rows, width = query.shape[1:]
    return pl.pallas_call(
        pack_kernel,
        out_shape=jax.ShapeDtypeStruct((width // HEAD_DIM, 3 * HEAD_DIM, rows), query.dtype),
        in_specs=vmem_specs(1),
        out_specs=pl.BlockSpec(memory_space=pltpu.VMEM),
        compiler_params=pltpu.CompilerParams(vmem_limit_bytes=4 * MIB),
        name="pack",
    )(jnp.concatenate([query, keys, values], axis=0))


def lanes(refs, lower, upper):
    return jnp.concatenate([ref[z, lower:upper, :] for ref in refs for z in range(ref.shape[0])], axis=1)


def block_steps(q_t, kv_refs, first, s_ref, p_ref, peak_old, emit):
    keys = lanes(kv_refs, first, first + HEAD_DIM).T
    v_t = lanes(kv_refs, first + HEAD_DIM, first + 2 * HEAD_DIM)
    v_aug = jnp.concatenate([v_t, jnp.ones((16, v_t.shape[1]), v_t.dtype)], axis=0)
    n = keys.shape[0]
    tiles = q_t.shape[1] // Q_TILE
    peaks = {}
    for step in range(tiles + 2):
        high = acc = None
        for lower in range(0, n, K_TILE):
            part = slice(lower, lower + K_TILE)
            if step < tiles:
                tile = slice(step * Q_TILE, (step + 1) * Q_TILE)
                s = jnp.dot(keys[part], q_t[:, tile], preferred_element_type=F32)
                s_ref[step % 2, part, :] = s
                top = jnp.max(s.reshape(K_TILE // 8, 8, Q_TILE), axis=0)
                high = top if high is None else jnp.maximum(high, top)
            if 0 <= step - 1 < tiles:
                expo = jnp.exp(s_ref[(step - 1) % 2, part, :] - peaks[step - 1])
                p_ref[(step - 1) % 2, part, :] = expo.astype(BF16)
            if 0 <= step - 2 < tiles:
                summed = jnp.dot(v_aug[:, part], p_ref[step % 2, part, :], preferred_element_type=F32)
                acc = summed if acc is None else acc + summed
        if step < tiles:
            peak = jnp.max(high, axis=0, keepdims=True)
            if peak_old is not None:
                peak = jnp.maximum(peak, peak_old[:, step * Q_TILE:(step + 1) * Q_TILE])
            peaks[step] = peak
        if step >= 2:
            emit(step - 2, peaks.pop(step - 2), acc)


def first_kernel(r_ref, peak_ref, acc_ref, s_ref, p_ref):
    def emit(tile, peak, acc):
        at = slice(tile * Q_TILE, (tile + 1) * Q_TILE)
        peak_ref[:, at] = peak
        acc_ref[:, at] = acc

    block_steps(lanes([r_ref], 0, HEAD_DIM), [r_ref], HEAD_DIM, s_ref, p_ref, None, emit)


def next_kernel(last, n_kv, r_ref, peak_ref, acc_ref, *refs):
    kv_refs, outs, (s_ref, p_ref) = refs[:n_kv], refs[n_kv:-2], refs[-2:]

    def emit(tile, peak, acc):
        at = slice(tile * Q_TILE, (tile + 1) * Q_TILE)
        acc = acc + acc_ref[:, at] * jnp.exp(peak_ref[:, at] - peak)
        if last:
            ctx = (acc[:HEAD_DIM] / acc[HEAD_DIM:HEAD_DIM + 1]).astype(BF16)
            rows = outs[0].shape[3]
            for j in range(Q_TILE // rows):
                for twin in range(2):
                    outs[0][tile * (Q_TILE // rows) + j, twin] = ctx[:, j * rows:(j + 1) * rows]
        else:
            outs[0][:, at] = peak
            outs[1][:, at] = acc

    block_steps(lanes([r_ref], 0, HEAD_DIM), kv_refs, 0, s_ref, p_ref, peak_ref[...], emit)


def attend_scratch(n):
    return [pltpu.VMEM((2, n, Q_TILE), F32), pltpu.VMEM((2, n, Q_TILE), BF16)]


def attend_first(r):
    n = r.shape[0] * r.shape[2]
    return pl.pallas_call(
        first_kernel,
        out_shape=(jax.ShapeDtypeStruct((1, n), F32), jax.ShapeDtypeStruct((HEAD_DIM + 16, n), F32)),
        in_specs=vmem_specs(1),
        out_specs=tuple(vmem_specs(2)),
        scratch_shapes=attend_scratch(n),
        compiler_params=pltpu.CompilerParams(vmem_limit_bytes=16 * MIB),
        name="attend_first",
    )(r)


def attend_next(r, kvs, peak, acc, last):
    n = r.shape[0] * r.shape[2]
    if last:
        shapes = (jax.ShapeDtypeStruct((r.shape[0], 2, HEAD_DIM, r.shape[2]), BF16),)
    else:
        shapes = (jax.ShapeDtypeStruct((1, n), F32), jax.ShapeDtypeStruct((HEAD_DIM + 16, n), F32))
    return pl.pallas_call(
        lambda *refs: next_kernel(last, len(kvs), *refs),
        out_shape=shapes,
        in_specs=vmem_specs(3 + len(kvs)),
        out_specs=tuple(vmem_specs(len(shapes))),
        scratch_shapes=attend_scratch(n),
        compiler_params=pltpu.CompilerParams(vmem_limit_bytes=16 * MIB),
        name="attend_last" if last else "attend_next",
    )(r, peak, acc, *kvs)


def unpack_kernel(at_ref, c_ref, o_ref):
    heads, _, dim, rows = c_ref.shape
    o_ref[0] = c_ref[:, at_ref[1] % 2].reshape(heads * dim, rows).T


def unpack(at, ctx_t):
    heads, _, dim, rows = ctx_t.shape
    return pl.pallas_call(
        unpack_kernel,
        out_shape=jax.ShapeDtypeStruct((1, rows, heads * dim), ctx_t.dtype),
        in_specs=[pl.BlockSpec(memory_space=pltpu.SMEM)] + vmem_specs(1),
        out_specs=pl.BlockSpec(memory_space=pltpu.VMEM),
        compiler_params=pltpu.CompilerParams(vmem_limit_bytes=4 * MIB),
        name="unpack",
    )(at, ctx_t)


def gather_rows(own):
    up = down = own
    pieces = [(own, 0)]
    for j in (1, 2, 3, 4):
        up = shift(up, "z", NZ, 1)
        pieces.append((up, j))
        if j < 4:
            down = shift(down, "z", NZ, -1)
            pieces.append((down, NZ - j))
    return pieces


def project_kernel(behind, at_ref, *refs):
    c0, c1, c3, c2a, c2b = refs[:5]
    ws = refs[5:5 + len(behind)]
    mine_ref, other_ref, ctx_ref, acc_ref = refs[5 + len(behind):]
    z, x, y = at_ref[0], at_ref[1], at_ref[2]
    _, _, dim, rows = c0.shape
    for d, parts in ((0, (c0,)), (1, (c1,)), (3, (c3,)), (2, (c2a, c2b))):
        group = (y + NY - d) % NY
        first = 0
        for part in parts:
            size = part.shape[0] * dim
            for twin in range(2):
                ctx_ref[group, first:first + size, twin * rows:(twin + 1) * rows] = part[:, twin].reshape(size, rows)
            first += size
    acc_ref[...] = jnp.zeros(acc_ref.shape, F32)
    strip = acc_ref.shape[2]
    for dz, w_ref in zip(behind, ws):
        zs = (z + NZ - dz) % NZ
        part = jnp.dot(w_ref[...].reshape(2 * strip, w_ref.shape[2]), ctx_ref[zs // 2], preferred_element_type=F32)
        acc_ref[zs % 2, x // 2] += part[:strip]
        acc_ref[zs % 2, 1 - x // 2] += part[strip:]
    for half in range(2):
        for i in range(2):
            left, right = acc_ref[half, i, :, :rows], acc_ref[half, i, :, rows:]
            second = x % 2 == 1
            mine_ref[half, i] = jnp.where(second, right, left)
            other_ref[half, i] = jnp.where(second, left, right).astype(BF16)


def project(at, contexts, pieces):
    behind = [dz for _, dz in pieces]
    rows = contexts[0].shape[3]
    strip = pieces[0][0].shape[1]
    return pl.pallas_call(
        lambda *refs: project_kernel(behind, *refs),
        out_shape=(
            jax.ShapeDtypeStruct((2, 2, strip, rows), F32),
            jax.ShapeDtypeStruct((2, 2, strip, rows), BF16),
        ),
        in_specs=[pl.BlockSpec(memory_space=pltpu.SMEM)] + vmem_specs(len(contexts) + len(pieces)),
        out_specs=tuple(vmem_specs(2)),
        scratch_shapes=[
            pltpu.VMEM((NY, 8 * HEAD_DIM, 2 * rows), BF16),
            pltpu.VMEM((2, 2, strip, 2 * rows), F32),
        ],
        compiler_params=pltpu.CompilerParams(vmem_limit_bytes=16 * MIB),
        name="project",
    )(at, *contexts, *[p[0] for p in pieces])


def add_kernel(strip, at_ref, mine_ref, other_ref, hidden_ref, o_ref, full_ref):
    second = at_ref[1] % 2
    for half in range(2):
        for x in range(NX):
            first = (half * NX + x) * strip
            mine, other = mine_ref[half, x // 2], other_ref[half, x // 2].astype(F32)
            full_ref[first:first + strip, :] = jnp.where(second == x % 2, mine, other)[:strip]
    o_ref[0] = (hidden_ref[0].astype(F32) + full_ref[...]).astype(o_ref.dtype)


def add_up(at, mine, other, hidden_t, strip):
    return pl.pallas_call(
        lambda *refs: add_kernel(strip, *refs),
        out_shape=jax.ShapeDtypeStruct(hidden_t.shape, hidden_t.dtype),
        in_specs=[pl.BlockSpec(memory_space=pltpu.SMEM)] + vmem_specs(3),
        out_specs=pl.BlockSpec(memory_space=pltpu.VMEM),
        scratch_shapes=[pltpu.VMEM(hidden_t.shape[1:], F32)],
        compiler_params=pltpu.CompilerParams(vmem_limit_bytes=8 * MIB),
        name="add_up",
    )(at, mine, other, hidden_t)


def layer(hidden, query, keys, values, w_out):
    at = jnp.stack([lax.axis_index("z"), lax.axis_index(X), lax.axis_index("mp")]).astype(jnp.int32)
    strip = w_out.shape[1]
    route = [
        ((s * NZ + z) * NY + y, ((1 - s) * NZ + 2 * y + z % 2) * NY + z // 2)
        for s in range(2) for z in range(NZ) for y in range(NY)
    ]
    here = lax.ppermute(w_out[0], ("section", "z", "mp"), route)
    here = jnp.pad(here, ((0, -strip % 8), (0, 0)))
    there = shift(here, X, NX, 2)
    pieces = gather_rows(jnp.stack([here, there]))
    hidden_t = lax.ppermute(jnp.swapaxes(hidden, 1, 2), "section", [(0, 1), (1, 0)])

    packed = pack(query, keys, values)
    r = lax.all_to_all(packed, "z", 0, 0, tiled=True)
    kv = r[:, HEAD_DIM:, :]
    half = NZ // 2
    kv1 = shift(kv, X, NX, 1)
    kv3 = shift(kv, X, NX, -1)
    kv2a = shift(kv1[:half], X, NX, 1)
    kv2b = shift(kv3[half:], X, NX, -1)
    peak, acc = attend_first(r)
    for j, kvs in enumerate(((kv1,), (kv3,), (kv2a, kv2b))):
        out = attend_next(r, kvs, peak, acc, j == 2)
        if j < 2:
            peak, acc = out

    sent = out[0].reshape((2 * NZ,) + out[0].shape[2:])
    own = lax.all_to_all(sent, ("z", "xl"), 0, 0, tiled=True).reshape(out[0].shape)

    def turned(by):
        turn = [(s * NY + y, (1 - s) * NY + (y + by) % NY) for s in range(2) for y in range(NY)]
        return lax.ppermute(own, ("section", "mp"), turn)

    ctx1 = turned(1)
    ctx3 = turned(-1)
    ctx0 = turned(0)
    ctx2a = shift(ctx1[:half], "mp", NY, 1)
    ctx2b = shift(ctx3[half:], "mp", NY, -1)
    context = unpack(at, own)
    mine, other = project(at, (ctx0, ctx1, ctx3, ctx2a, ctx2b), pieces)
    other = lax.ppermute(other, "xl", [(0, 1), (1, 0)])
    handed_t = add_up(at, mine, other, hidden_t, strip)
    return jnp.swapaxes(handed_t, 1, 2), context


def solution(mesh):
    split = Mesh(mesh.devices.reshape(2, NZ, NX // 2, 2, NY), ("section", "z") + X + ("mp",))
    spec = P("section", ("z",) + X, "mp")
    return jax.shard_map(layer, mesh=split, in_specs=(spec,) * 5, out_specs=(spec, spec), check_vma=False)
```

```python
import jax
import jax.numpy as jnp
from jax import lax
from jax.experimental import pallas as pl
from jax.experimental.pallas import tpu as pltpu
from jax.sharding import Mesh, PartitionSpec as P


HEAD_DIM = 64
NZ, NX, NY = 8, 4, 4
X = ("xh", "xl")
Q_TILE = 256
K_TILE = 256


F32 = jnp.float32
BF16 = jnp.bfloat16
MIB = 1 << 20


def vmem_specs(n):
    return [pl.BlockSpec(memory_space=pltpu.VMEM) for _ in range(n)]


def shift(block, axis, n, by):
    return lax.ppermute(block, axis, [(i, (i + by) % n) for i in range(n)])


def pack_kernel(in_ref, o_ref):
    for i in range(3):
        t = in_ref[i].T
        heads = t.shape[0] // HEAD_DIM
        o_ref[:, i * HEAD_DIM:(i + 1) * HEAD_DIM, :] = t.reshape(heads, HEAD_DIM, t.shape[1])


def pack(query, keys, values):
    rows, width = query.shape[1:]
    return pl.pallas_call(
        pack_kernel,
        out_shape=jax.ShapeDtypeStruct((width // HEAD_DIM, 3 * HEAD_DIM, rows), query.dtype),
        in_specs=vmem_specs(1),
        out_specs=pl.BlockSpec(memory_space=pltpu.VMEM),
        compiler_params=pltpu.CompilerParams(vmem_limit_bytes=4 * MIB),
        name="pack",
    )(jnp.concatenate([query, keys, values], axis=0))


def lanes(refs, lower, upper):
    return jnp.concatenate([ref[z, lower:upper, :] for ref in refs for z in range(ref.shape[0])], axis=1)


def block_steps(q_t, kv_refs, first, s_ref, p_ref, peak_old, emit):
    keys = lanes(kv_refs, first, first + HEAD_DIM).T
    v_t = lanes(kv_refs, first + HEAD_DIM, first + 2 * HEAD_DIM)
    v_aug = jnp.concatenate([v_t, jnp.ones((16, v_t.shape[1]), v_t.dtype)], axis=0)
    n = keys.shape[0]
    tiles = q_t.shape[1] // Q_TILE
    peaks = {}
    for step in range(tiles + 2):
        high = acc = None
        for lower in range(0, n, K_TILE):
            part = slice(lower, lower + K_TILE)
            if step < tiles:
                tile = slice(step * Q_TILE, (step + 1) * Q_TILE)
                s = jnp.dot(keys[part], q_t[:, tile], preferred_element_type=F32)
                s_ref[step % 2, part, :] = s
                top = jnp.max(s.reshape(K_TILE // 8, 8, Q_TILE), axis=0)
                high = top if high is None else jnp.maximum(high, top)
            if 0 <= step - 1 < tiles:
                expo = jnp.exp(s_ref[(step - 1) % 2, part, :] - peaks[step - 1])
                p_ref[(step - 1) % 2, part, :] = expo.astype(BF16)
            if 0 <= step - 2 < tiles:
                summed = jnp.dot(v_aug[:, part], p_ref[step % 2, part, :], preferred_element_type=F32)
                acc = summed if acc is None else acc + summed
        if step < tiles:
            peak = jnp.max(high, axis=0, keepdims=True)
            if peak_old is not None:
                peak = jnp.maximum(peak, peak_old[:, step * Q_TILE:(step + 1) * Q_TILE])
            peaks[step] = peak
        if step >= 2:
            emit(step - 2, peaks.pop(step - 2), acc)


def first_kernel(r_ref, peak_ref, acc_ref, s_ref, p_ref):
    def emit(tile, peak, acc):
        at = slice(tile * Q_TILE, (tile + 1) * Q_TILE)
        peak_ref[:, at] = peak
        acc_ref[:, at] = acc

    block_steps(lanes([r_ref], 0, HEAD_DIM), [r_ref], HEAD_DIM, s_ref, p_ref, None, emit)


def next_kernel(last, n_kv, r_ref, peak_ref, acc_ref, *refs):
    kv_refs, outs, (s_ref, p_ref) = refs[:n_kv], refs[n_kv:-2], refs[-2:]

    def emit(tile, peak, acc):
        at = slice(tile * Q_TILE, (tile + 1) * Q_TILE)
        acc = acc + acc_ref[:, at] * jnp.exp(peak_ref[:, at] - peak)
        if last:
            ctx = (acc[:HEAD_DIM] / acc[HEAD_DIM:HEAD_DIM + 1]).astype(BF16)
            rows = outs[0].shape[3]
            for j in range(Q_TILE // rows):
                for twin in range(2):
                    outs[0][tile * (Q_TILE // rows) + j, twin] = ctx[:, j * rows:(j + 1) * rows]
        else:
            outs[0][:, at] = peak
            outs[1][:, at] = acc

    block_steps(lanes([r_ref], 0, HEAD_DIM), kv_refs, 0, s_ref, p_ref, peak_ref[...], emit)


def attend_scratch(n):
    return [pltpu.VMEM((2, n, Q_TILE), F32), pltpu.VMEM((2, n, Q_TILE), BF16)]


def attend_first(r):
    n = r.shape[0] * r.shape[2]
    return pl.pallas_call(
        first_kernel,
        out_shape=(jax.ShapeDtypeStruct((1, n), F32), jax.ShapeDtypeStruct((HEAD_DIM + 16, n), F32)),
        in_specs=vmem_specs(1),
        out_specs=tuple(vmem_specs(2)),
        scratch_shapes=attend_scratch(n),
        compiler_params=pltpu.CompilerParams(vmem_limit_bytes=16 * MIB),
        name="attend_first",
    )(r)


def attend_next(r, kvs, peak, acc, last):
    n = r.shape[0] * r.shape[2]
    if last:
        shapes = (jax.ShapeDtypeStruct((r.shape[0], 2, HEAD_DIM, r.shape[2]), BF16),)
    else:
        shapes = (jax.ShapeDtypeStruct((1, n), F32), jax.ShapeDtypeStruct((HEAD_DIM + 16, n), F32))
    return pl.pallas_call(
        lambda *refs: next_kernel(last, len(kvs), *refs),
        out_shape=shapes,
        in_specs=vmem_specs(3 + len(kvs)),
        out_specs=tuple(vmem_specs(len(shapes))),
        scratch_shapes=attend_scratch(n),
        compiler_params=pltpu.CompilerParams(vmem_limit_bytes=16 * MIB),
        name="attend_last" if last else "attend_next",
    )(r, peak, acc, *kvs)


def unpack_kernel(at_ref, c_ref, o_ref):
    heads, _, dim, rows = c_ref.shape
    o_ref[0] = c_ref[:, at_ref[1] % 2].reshape(heads * dim, rows).T


def unpack(at, ctx_t):
    heads, _, dim, rows = ctx_t.shape
    return pl.pallas_call(
        unpack_kernel,
        out_shape=jax.ShapeDtypeStruct((1, rows, heads * dim), ctx_t.dtype),
        in_specs=[pl.BlockSpec(memory_space=pltpu.SMEM)] + vmem_specs(1),
        out_specs=pl.BlockSpec(memory_space=pltpu.VMEM),
        compiler_params=pltpu.CompilerParams(vmem_limit_bytes=4 * MIB),
        name="unpack",
    )(at, ctx_t)


def gather_rows(own):
    up = down = own
    pieces = [(own, 0)]
    for j in (1, 2, 3, 4):
        up = shift(up, "z", NZ, 1)
        pieces.append((up, j))
        if j < 4:
            down = shift(down, "z", NZ, -1)
            pieces.append((down, NZ - j))
    return pieces


def project_kernel(behind, at_ref, *refs):
    c0, c1a, c1b, c3a, c3b, c2a, c2b = refs[:7]
    ws = refs[7:-4]
    mine_ref, other_ref, ctx_ref, acc_ref = refs[-4:]
    z, x, y = at_ref[0], at_ref[1], at_ref[2]
    _, _, dim, rows = c0.shape
    for d, parts in ((0, (c0,)), (1, (c1a, c1b)), (3, (c3a, c3b)), (2, (c2a, c2b))):
        group = (y + NY - d) % NY
        first = 0
        for part in parts:
            size = part.shape[0] * dim
            for twin in range(2):
                ctx_ref[group, first:first + size, twin * rows:(twin + 1) * rows] = part[:, twin].reshape(size, rows)
            first += size
    acc_ref[...] = jnp.zeros(acc_ref.shape, F32)
    strip = acc_ref.shape[2]
    for dz, w_ref in zip(behind, ws):
        zs = (z + NZ - dz) % NZ
        part = jnp.dot(w_ref[...].reshape(2 * strip, w_ref.shape[2]), ctx_ref[zs // 2], preferred_element_type=F32)
        acc_ref[zs % 2, x // 2] += part[:strip]
        acc_ref[zs % 2, 1 - x // 2] += part[strip:]
    for half in range(2):
        for i in range(2):
            left, right = acc_ref[half, i, :, :rows], acc_ref[half, i, :, rows:]
            second = x % 2 == 1
            mine_ref[half, i] = jnp.where(second, right, left)
            other_ref[half, i] = jnp.where(second, left, right).astype(BF16)


def project(at, contexts, pieces):
    behind = [dz for _, dz in pieces]
    rows = contexts[0].shape[3]
    strip = pieces[0][0].shape[1]
    return pl.pallas_call(
        lambda *refs: project_kernel(behind, *refs),
        out_shape=(
            jax.ShapeDtypeStruct((2, 2, strip, rows), F32),
            jax.ShapeDtypeStruct((2, 2, strip, rows), BF16),
        ),
        in_specs=[pl.BlockSpec(memory_space=pltpu.SMEM)] + vmem_specs(len(contexts) + len(pieces)),
        out_specs=tuple(vmem_specs(2)),
        scratch_shapes=[
            pltpu.VMEM((NY, 8 * HEAD_DIM, 2 * rows), BF16),
            pltpu.VMEM((2, 2, strip, 2 * rows), F32),
        ],
        compiler_params=pltpu.CompilerParams(vmem_limit_bytes=16 * MIB),
        name="project",
    )(at, *contexts, *[p[0] for p in pieces])


def add_kernel(strip, at_ref, mine_ref, other_ref, hidden_ref, o_ref, full_ref):
    second = at_ref[1] % 2
    for half in range(2):
        for x in range(NX):
            first = (half * NX + x) * strip
            mine, other = mine_ref[half, x // 2], other_ref[half, x // 2].astype(F32)
            full_ref[first:first + strip, :] = jnp.where(second == x % 2, mine, other)[:strip]
    o_ref[0] = (hidden_ref[0].astype(F32) + full_ref[...]).astype(o_ref.dtype)


def add_up(at, mine, other, hidden_t, strip):
    return pl.pallas_call(
        lambda *refs: add_kernel(strip, *refs),
        out_shape=jax.ShapeDtypeStruct(hidden_t.shape, hidden_t.dtype),
        in_specs=[pl.BlockSpec(memory_space=pltpu.SMEM)] + vmem_specs(3),
        out_specs=pl.BlockSpec(memory_space=pltpu.VMEM),
        scratch_shapes=[pltpu.VMEM(hidden_t.shape[1:], F32)],
        compiler_params=pltpu.CompilerParams(vmem_limit_bytes=8 * MIB),
        name="add_up",
    )(at, mine, other, hidden_t)


def layer(hidden, query, keys, values, w_out):
    at = jnp.stack([lax.axis_index("z"), lax.axis_index(X), lax.axis_index("mp")]).astype(jnp.int32)
    strip = w_out.shape[1]
    route = [
        ((s * NZ + z) * NY + y, ((1 - s) * NZ + 2 * y + z % 2) * NY + z // 2)
        for s in range(2) for z in range(NZ) for y in range(NY)
    ]
    here = lax.ppermute(w_out[0], ("section", "z", "mp"), route)
    here = jnp.pad(here, ((0, -strip % 8), (0, 0)))
    there = shift(here, X, NX, 2)
    pieces = gather_rows(jnp.stack([here, there]))
    hidden_t = lax.ppermute(jnp.swapaxes(hidden, 1, 2), "section", [(0, 1), (1, 0)])

    packed = pack(query, keys, values)
    r = lax.all_to_all(packed, "z", 0, 0, tiled=True)
    half = NZ // 2
    low, high = r[:half, HEAD_DIM:, :], r[half:, HEAD_DIM:, :]
    kv1a = shift(low, X, NX, 1)
    kv3b = shift(high, X, NX, -1)
    kv1b = shift(high, X, NX, 1)
    kv3a = shift(low, X, NX, -1)
    kv2a = shift(kv1a, X, NX, 1)
    kv2b = shift(kv3b, X, NX, -1)
    peak, acc = attend_first(r)
    for j, kvs in enumerate(((kv1a, kv1b), (kv3a, kv3b), (kv2a, kv2b))):
        out = attend_next(r, kvs, peak, acc, j == 2)
        if j < 2:
            peak, acc = out

    sent = out[0].reshape((2 * NZ,) + out[0].shape[2:])
    own = lax.all_to_all(sent, ("z", "xl"), 0, 0, tiled=True).reshape(out[0].shape)

    def turned(block, by):
        turn = [(s * NY + y, (1 - s) * NY + (y + by) % NY) for s in range(2) for y in range(NY)]
        return lax.ppermute(block, ("section", "mp"), turn)

    low, high = own[:half], own[half:]
    ctx1a = turned(low, 1)
    ctx3b = turned(high, -1)
    ctx1b = turned(high, 1)
    ctx3a = turned(low, -1)
    ctx0 = turned(own, 0)
    ctx2a = shift(ctx1a, "mp", NY, 1)
    ctx2b = shift(ctx3b, "mp", NY, -1)
    context = unpack(at, own)
    mine, other = project(at, (ctx0, ctx1a, ctx1b, ctx3a, ctx3b, ctx2a, ctx2b), pieces)
    other = lax.ppermute(other, "xl", [(0, 1), (1, 0)])
    handed_t = add_up(at, mine, other, hidden_t, strip)
    return jnp.swapaxes(handed_t, 1, 2), context


def solution(mesh):
    split = Mesh(mesh.devices.reshape(2, NZ, NX // 2, 2, NY), ("section", "z") + X + ("mp",))
    spec = P("section", ("z",) + X, "mp")
    return jax.shard_map(layer, mesh=split, in_specs=(spec,) * 5, out_specs=(spec, spec), check_vma=False)
```

```python
import jax
import jax.numpy as jnp
from jax import lax
from jax.experimental import pallas as pl
from jax.experimental.pallas import tpu as pltpu
from jax.sharding import Mesh, PartitionSpec as P


HEAD_DIM = 64
NZ, NX, NY = 8, 4, 4
X = ("xh", "xl")
Q_TILE = 256
K_TILE = 256


F32 = jnp.float32
BF16 = jnp.bfloat16
MIB = 1 << 20


def vmem_specs(n):
    return [pl.BlockSpec(memory_space=pltpu.VMEM) for _ in range(n)]


def shift(block, axis, n, by):
    return lax.ppermute(block, axis, [(i, (i + by) % n) for i in range(n)])


def pack_kernel(in_ref, o_ref):
    for i in range(3):
        t = in_ref[i].T
        heads = t.shape[0] // HEAD_DIM
        o_ref[:, i * HEAD_DIM:(i + 1) * HEAD_DIM, :] = t.reshape(heads, HEAD_DIM, t.shape[1])


def pack(query, keys, values):
    rows, width = query.shape[1:]
    return pl.pallas_call(
        pack_kernel,
        out_shape=jax.ShapeDtypeStruct((width // HEAD_DIM, 3 * HEAD_DIM, rows), query.dtype),
        in_specs=vmem_specs(1),
        out_specs=pl.BlockSpec(memory_space=pltpu.VMEM),
        compiler_params=pltpu.CompilerParams(vmem_limit_bytes=4 * MIB),
        name="pack",
    )(jnp.concatenate([query, keys, values], axis=0))


def lanes(refs, lower, upper):
    return jnp.concatenate([ref[z, lower:upper, :] for ref in refs for z in range(ref.shape[0])], axis=1)


def block_steps(q_t, kv_refs, first, s_ref, p_ref, peak_old, emit):
    keys = lanes(kv_refs, first, first + HEAD_DIM).T
    v_t = lanes(kv_refs, first + HEAD_DIM, first + 2 * HEAD_DIM)
    v_aug = jnp.concatenate([v_t, jnp.ones((16, v_t.shape[1]), v_t.dtype)], axis=0)
    n = keys.shape[0]
    tiles = q_t.shape[1] // Q_TILE
    peaks = {}
    for step in range(tiles + 2):
        high = acc = None
        for lower in range(0, n, K_TILE):
            part = slice(lower, lower + K_TILE)
            if step < tiles:
                tile = slice(step * Q_TILE, (step + 1) * Q_TILE)
                s = jnp.dot(keys[part], q_t[:, tile], preferred_element_type=F32)
                s_ref[step % 2, part, :] = s
                top = jnp.max(s.reshape(K_TILE // 8, 8, Q_TILE), axis=0)
                high = top if high is None else jnp.maximum(high, top)
            if 0 <= step - 1 < tiles:
                expo = jnp.exp(s_ref[(step - 1) % 2, part, :] - peaks[step - 1])
                p_ref[(step - 1) % 2, part, :] = expo.astype(BF16)
            if 0 <= step - 2 < tiles:
                summed = jnp.dot(v_aug[:, part], p_ref[step % 2, part, :], preferred_element_type=F32)
                acc = summed if acc is None else acc + summed
        if step < tiles:
            peak = jnp.max(high, axis=0, keepdims=True)
            if peak_old is not None:
                peak = jnp.maximum(peak, peak_old[:, step * Q_TILE:(step + 1) * Q_TILE])
            peaks[step] = peak
        if step >= 2:
            emit(step - 2, peaks.pop(step - 2), acc)


def first_kernel(r_ref, peak_ref, acc_ref, s_ref, p_ref):
    def emit(tile, peak, acc):
        at = slice(tile * Q_TILE, (tile + 1) * Q_TILE)
        peak_ref[:, at] = peak
        acc_ref[:, at] = acc

    block_steps(lanes([r_ref], 0, HEAD_DIM), [r_ref], HEAD_DIM, s_ref, p_ref, None, emit)


def next_kernel(last, n_kv, r_ref, peak_ref, acc_ref, *refs):
    kv_refs, outs, (s_ref, p_ref) = refs[:n_kv], refs[n_kv:-2], refs[-2:]

    def emit(tile, peak, acc):
        at = slice(tile * Q_TILE, (tile + 1) * Q_TILE)
        acc = acc + acc_ref[:, at] * jnp.exp(peak_ref[:, at] - peak)
        if last:
            ctx = (acc[:HEAD_DIM] / acc[HEAD_DIM:HEAD_DIM + 1]).astype(BF16)
            rows = outs[0].shape[3]
            for j in range(Q_TILE // rows):
                for twin in range(2):
                    outs[0][tile * (Q_TILE // rows) + j, twin] = ctx[:, j * rows:(j + 1) * rows]
        else:
            outs[0][:, at] = peak
            outs[1][:, at] = acc

    block_steps(lanes([r_ref], 0, HEAD_DIM), kv_refs, 0, s_ref, p_ref, peak_ref[...], emit)


def attend_scratch(n):
    return [pltpu.VMEM((2, n, Q_TILE), F32), pltpu.VMEM((2, n, Q_TILE), BF16)]


def attend_first(r):
    n = r.shape[0] * r.shape[2]
    return pl.pallas_call(
        first_kernel,
        out_shape=(jax.ShapeDtypeStruct((1, n), F32), jax.ShapeDtypeStruct((HEAD_DIM + 16, n), F32)),
        in_specs=vmem_specs(1),
        out_specs=tuple(vmem_specs(2)),
        scratch_shapes=attend_scratch(n),
        compiler_params=pltpu.CompilerParams(vmem_limit_bytes=16 * MIB),
        name="attend_first",
    )(r)


def attend_next(r, kvs, peak, acc, last):
    n = r.shape[0] * r.shape[2]
    if last:
        shapes = (jax.ShapeDtypeStruct((r.shape[0], 2, HEAD_DIM, r.shape[2]), BF16),)
    else:
        shapes = (jax.ShapeDtypeStruct((1, n), F32), jax.ShapeDtypeStruct((HEAD_DIM + 16, n), F32))
    return pl.pallas_call(
        lambda *refs: next_kernel(last, len(kvs), *refs),
        out_shape=shapes,
        in_specs=vmem_specs(3 + len(kvs)),
        out_specs=tuple(vmem_specs(len(shapes))),
        scratch_shapes=attend_scratch(n),
        compiler_params=pltpu.CompilerParams(vmem_limit_bytes=16 * MIB),
        name="attend_last" if last else "attend_next",
    )(r, peak, acc, *kvs)


def unpack_kernel(at_ref, c_ref, o_ref):
    heads, _, dim, rows = c_ref.shape
    o_ref[0] = c_ref[:, at_ref[1] % 2].reshape(heads * dim, rows).T


def unpack(at, ctx_t):
    heads, _, dim, rows = ctx_t.shape
    return pl.pallas_call(
        unpack_kernel,
        out_shape=jax.ShapeDtypeStruct((1, rows, heads * dim), ctx_t.dtype),
        in_specs=[pl.BlockSpec(memory_space=pltpu.SMEM)] + vmem_specs(1),
        out_specs=pl.BlockSpec(memory_space=pltpu.VMEM),
        compiler_params=pltpu.CompilerParams(vmem_limit_bytes=4 * MIB),
        name="unpack",
    )(at, ctx_t)


def gather_rows(own):
    up = down = own
    pieces = [(own, 0)]
    for j in (1, 2, 3, 4):
        up = shift(up, "z", NZ, 1)
        pieces.append((up, j))
        if j < 4:
            down = shift(down, "z", NZ, -1)
            pieces.append((down, NZ - j))
    return pieces


def project_kernel(other, behind, at_ref, *refs):
    c0, c1a, c1b, c3a, c3b, c2a, c2b = refs[:7]
    ws = refs[7:-3]
    o_ref, ctx_ref, acc_ref = refs[-3:]
    z, x, y = at_ref[0], at_ref[1], at_ref[2]
    twin = 1 - x % 2 if other else x % 2
    for d, parts in ((0, (c0,)), (1, (c1a, c1b)), (3, (c3a, c3b)), (2, (c2a, c2b))):
        group = (y + NY - d) % NY
        first = 0
        for part in parts:
            size = part.shape[0] * part.shape[2]
            ctx_ref[group, first:first + size, :] = part[:, twin].reshape(size, part.shape[3])
            first += size
    acc_ref[...] = jnp.zeros(acc_ref.shape, F32)
    strip = acc_ref.shape[2]
    for dz, w_ref in zip(behind, ws):
        zs = (z + NZ - dz) % NZ
        part = jnp.dot(w_ref[...].reshape(2 * strip, w_ref.shape[2]), ctx_ref[zs // 2], preferred_element_type=F32)
        acc_ref[zs % 2, x // 2] += part[:strip]
        acc_ref[zs % 2, 1 - x // 2] += part[strip:]
    o_ref[...] = acc_ref[...].astype(o_ref.dtype)


def project(at, contexts, pieces, other):
    behind = [dz for _, dz in pieces]
    rows = contexts[0].shape[3]
    strip = pieces[0][0].shape[1]
    return pl.pallas_call(
        lambda *refs: project_kernel(other, behind, *refs),
        out_shape=jax.ShapeDtypeStruct((2, 2, strip, rows), BF16 if other else F32),
        in_specs=[pl.BlockSpec(memory_space=pltpu.SMEM)] + vmem_specs(len(contexts) + len(pieces)),
        out_specs=pl.BlockSpec(memory_space=pltpu.VMEM),
        scratch_shapes=[pltpu.VMEM((NY, 8 * HEAD_DIM, rows), BF16), pltpu.VMEM((2, 2, strip, rows), F32)],
        compiler_params=pltpu.CompilerParams(vmem_limit_bytes=16 * MIB),
        name="project_other" if other else "project_mine",
    )(at, *contexts, *[p[0] for p in pieces])


def add_kernel(strip, at_ref, mine_ref, other_ref, hidden_ref, o_ref, full_ref):
    second = at_ref[1] % 2
    for half in range(2):
        for x in range(NX):
            first = (half * NX + x) * strip
            mine, other = mine_ref[half, x // 2], other_ref[half, x // 2].astype(F32)
            full_ref[first:first + strip, :] = jnp.where(second == x % 2, mine, other)[:strip]
    o_ref[0] = (hidden_ref[0].astype(F32) + full_ref[...]).astype(o_ref.dtype)


def add_up(at, mine, other, hidden_t, strip):
    return pl.pallas_call(
        lambda *refs: add_kernel(strip, *refs),
        out_shape=jax.ShapeDtypeStruct(hidden_t.shape, hidden_t.dtype),
        in_specs=[pl.BlockSpec(memory_space=pltpu.SMEM)] + vmem_specs(3),
        out_specs=pl.BlockSpec(memory_space=pltpu.VMEM),
        scratch_shapes=[pltpu.VMEM(hidden_t.shape[1:], F32)],
        compiler_params=pltpu.CompilerParams(vmem_limit_bytes=8 * MIB),
        name="add_up",
    )(at, mine, other, hidden_t)


def layer(hidden, query, keys, values, w_out):
    at = jnp.stack([lax.axis_index("z"), lax.axis_index(X), lax.axis_index("mp")]).astype(jnp.int32)
    strip = w_out.shape[1]
    route = [
        ((s * NZ + z) * NY + y, ((1 - s) * NZ + 2 * y + z % 2) * NY + z // 2)
        for s in range(2) for z in range(NZ) for y in range(NY)
    ]
    here = lax.ppermute(w_out[0], ("section", "z", "mp"), route)
    here = jnp.pad(here, ((0, -strip % 8), (0, 0)))
    there = shift(here, X, NX, 2)
    pieces = gather_rows(jnp.stack([here, there]))
    hidden_t = lax.ppermute(jnp.swapaxes(hidden, 1, 2), "section", [(0, 1), (1, 0)])

    packed = pack(query, keys, values)
    r = lax.all_to_all(packed, "z", 0, 0, tiled=True)
    half = NZ // 2
    low, high = r[:half, HEAD_DIM:, :], r[half:, HEAD_DIM:, :]
    kv1a = shift(low, X, NX, 1)
    kv3b = shift(high, X, NX, -1)
    kv1b = shift(high, X, NX, 1)
    kv3a = shift(low, X, NX, -1)
    kv2a = shift(kv1a, X, NX, 1)
    kv2b = shift(kv3b, X, NX, -1)
    peak, acc = attend_first(r)
    for j, kvs in enumerate(((kv1a, kv1b), (kv3a, kv3b), (kv2a, kv2b))):
        out = attend_next(r, kvs, peak, acc, j == 2)
        if j < 2:
            peak, acc = out

    sent = out[0].reshape((2 * NZ,) + out[0].shape[2:])
    own = lax.all_to_all(sent, ("z", "xl"), 0, 0, tiled=True).reshape(out[0].shape)

    def turned(block, by):
        turn = [(s * NY + y, (1 - s) * NY + (y + by) % NY) for s in range(2) for y in range(NY)]
        return lax.ppermute(block, ("section", "mp"), turn)

    low, high = own[:half], own[half:]
    ctx1a = turned(low, 1)
    ctx3b = turned(high, -1)
    ctx1b = turned(high, 1)
    ctx3a = turned(low, -1)
    ctx0 = turned(own, 0)
    ctx2a = shift(ctx1a, "mp", NY, 1)
    ctx2b = shift(ctx3b, "mp", NY, -1)
    context = unpack(at, own)
    contexts = (ctx0, ctx1a, ctx1b, ctx3a, ctx3b, ctx2a, ctx2b)
    other = project(at, contexts, pieces, True)
    mine = project(at, contexts, pieces, False)
    other = lax.ppermute(other, "xl", [(0, 1), (1, 0)])
    handed_t = add_up(at, mine, other, hidden_t, strip)
    return jnp.swapaxes(handed_t, 1, 2), context


def solution(mesh):
    split = Mesh(mesh.devices.reshape(2, NZ, NX // 2, 2, NY), ("section", "z") + X + ("mp",))
    spec = P("section", ("z",) + X, "mp")
    return jax.shard_map(layer, mesh=split, in_specs=(spec,) * 5, out_specs=(spec, spec), check_vma=False)
```
